32 devices in a mesh: grp: 16 (over z, y, core), chan: 2 (over x).
Axes of the slice: x: 2, y: 2, z: 4, core: 2. Of those that a mesh axis runs over, the one named last changes fastest.
Arguments:
- voltages: bfloat16 [32, 2, 4096, 256], P(None, None, 'grp', 'chan'), may hold values from -6 to 6
- input_flags: int32 [4096], P('grp'), may hold values 0 or 1
- pair_order: int32 [9], replicated, may hold values from 0 to 8, each once
Outputs:
- visibilities: float32 [16, 9, 32, 256, 512], P('grp', None, 'chan')
The draws below stay inside these ranges and needn't reach their ends.
Inputs may be any that keep to these rules, and one draw needn't show every extreme that they name: `pair_order`: a permutation of 0 to 8.
All inputs are finite; a program needn't handle non-finite values. No bound on the sum of `input_flags` on one device may be relied on, other than what follows from the above.
Results may differ from the reference program's by a relative error of at most 0.0003.
Values may be sent and summed in bfloat16 or wider, within the bound.
No kernel may reach another device: no remote copies, remote signals or barrier semaphores. Data moves between devices by JAX's collectives and lax.ppermute only.
A program may use at most 320 MiB of HBM per device.

```python
import jax
import jax.numpy as jnp
from jax import lax

NIN = 4096
CH = 32
SPECTRA = 256
GROUPS = 16
GS = 256
SLOTS = 9


def with_ends(values, own_key, least, top_value):
    dims = values.shape
    place = [jax.random.randint(jax.random.fold_in(own_key, axis), (), 0, dims[axis]) for axis in range(len(dims))]
    values = values.at[tuple(place)].set(least)
    longest = dims.index(max(dims))
    place[longest] = (place[longest] + 1) % dims[longest]
    return values.at[tuple(place)].set(top_value)


def shard_levels(own_key, shape, split, low, top_value):
    gain, own = 1.0, jax.random.fold_in(own_key, 6)
    for axis_at, parts in split:
        draws = jnp.exp(jax.random.uniform(jax.random.fold_in(own, axis_at), (parts,), jnp.float32, low / len(split), top_value / len(split)))
        gain = gain * jnp.repeat(draws, shape[axis_at] // parts).reshape([-1 if axis == axis_at else 1 for axis in range(len(shape))])
    return gain


def bell_draw(rng, extent, deviation, most, pieces=(), held_as=jnp.bfloat16):
    factor_of = shard_levels(rng, extent, pieces, -0.22, 0.18) if pieces else 1.0
    entries = jax.random.normal(rng, extent, jnp.float32) * deviation * factor_of
    return jnp.minimum(jnp.maximum(entries, -most), most).astype(held_as)


def setup_inputs(seed: int = 0) -> dict:
    arg_keys = jax.random.split(jax.random.key(seed), 4)
    return {
        "voltages": bell_draw(arg_keys[0], (CH, 2, NIN, SPECTRA), 1.0, 6.0, ((2, 16), (3, 2))),
        "input_flags": with_ends((jax.random.randint(arg_keys[1], (NIN,), 0, 8) < 7).astype(jnp.int32), jax.random.fold_in(arg_keys[1], 1), 0, 1),
        "pair_order": jax.random.permutation(arg_keys[2], SLOTS).astype(jnp.int32),
    }


def correlate(rows, cols):
    products = jnp.einsum("cpgit,cugjt->gcipuj", rows, cols, precision=lax.Precision.HIGHEST)
    real_part = products[:, :, :, 0, 0] + products[:, :, :, 1, 1]
    imag_part = products[:, :, :, 1, 0] - products[:, :, :, 0, 1]
    return jnp.concatenate([real_part, imag_part], axis=-1)


def reference(voltages, input_flags, pair_order):
    signal = voltages.astype(jnp.float32) * input_flags.astype(jnp.float32)[None, None, :, None]
    grouped = signal.reshape(CH, 2, GROUPS, GS, SPECTRA)
    tiles = []
    for offset in range(SLOTS):
        rows = jnp.roll(grouped, offset // 2, axis=2)
        cols = jnp.roll(grouped, -((offset + 1) // 2), axis=2)
        tiles.append(correlate(rows, cols) * jnp.float32(1.0 / SPECTRA))
    stacked = jnp.stack(tiles, axis=1)
    return jnp.zeros_like(stacked).at[:, pair_order].set(stacked)
```

```python
import functools

import jax
import jax.numpy as jnp
from jax import lax
from jax.experimental import pallas as pl
from jax.experimental.pallas import tpu as pltpu
from jax.sharding import PartitionSpec as P


def pair_kernel(variants, parts, blocks, table, *refs):
    width = len(variants[0])
    sources = refs[:blocks]
    out, window, sems = refs[-3:]
    step = pl.program_id(0)
    steps = pl.num_programs(0)

    def copy(source, channel, slot, entry, part):
        return pltpu.make_async_copy(
            sources[source * parts + part].at[channel],
            window.at[slot, entry, part],
            sems.at[slot, entry, part],
        )

    def fetch(channel, slot):
        for at, variant in enumerate(variants):

            @pl.when(table[0] == at)
            def _():
                for entry, source in enumerate(variant):
                    for part in range(parts):
                        copy(source, channel, slot, entry, part).start()

    @pl.when(step == 0)
    def _():
        fetch(0, 0)

    @pl.when(step + 1 < steps)
    def _():
        fetch(step + 1, lax.rem(step + 1, 2))

    slot = lax.rem(step, 2)
    for entry in range(width):
        for part in range(parts):
            copy(0, 0, slot, entry, part).wait()

    half = width // 2
    size = window.shape[-2]
    scale = jnp.float32(1.0 / (parts * window.shape[-1]))
    contract = (((1,), (1,)), ((), ()))

    def pair(d, carry):
        a = half - d // 2
        b = half + (d + 1) // 2
        real = jnp.zeros((size, size), jnp.float32)
        imag = jnp.zeros((size, size), jnp.float32)
        for part in range(parts):
            left = jnp.concatenate([window[slot, a, part, 0], window[slot, a, part, 1]], axis=1)
            b_r, b_i = window[slot, b, part, 0], window[slot, b, part, 1]
            real = real + lax.dot_general(
                left, jnp.concatenate([b_r, b_i], axis=1), contract, preferred_element_type=jnp.float32
            )
            imag = imag + lax.dot_general(
                left, jnp.concatenate([-b_i, b_r], axis=1), contract, preferred_element_type=jnp.float32
            )
        to = table[1 + d]
        out[0, to, 0, :, :size] = real * scale
        out[0, to, 0, :, size:] = imag * scale
        return carry

    if width <= 9:
        for d in range(width):
            pair(d, 0)
    else:
        lax.fori_loop(0, width, pair, 0)


def correlate(sources, parts, variants, table, first, channels, previous):
    count, _, size, samples = sources[0].shape
    width = len(variants[0])
    out_shape = (1, width, channels, size, 2 * size)
    operands = list(sources) + ([] if previous is None else [previous])
    return pl.pallas_call(
        functools.partial(pair_kernel, variants, parts, len(sources)),
        out_shape=jax.ShapeDtypeStruct(out_shape, jnp.float32),
        grid_spec=pltpu.PrefetchScalarGridSpec(
            num_scalar_prefetch=1,
            grid=(count,),
            in_specs=[pl.BlockSpec(memory_space=pl.ANY)] * len(operands),
            out_specs=pl.BlockSpec((1, width, 1, size, 2 * size), lambda c, t: (0, 0, first + c, 0, 0)),
            scratch_shapes=[
                pltpu.VMEM((2, width, parts, 2, size, samples), jnp.bfloat16),
                pltpu.SemaphoreType.DMA((2, width, parts)),
            ],
        ),
        input_output_aliases={} if previous is None else {len(operands): 0},
        compiler_params=pltpu.CompilerParams(
            dimension_semantics=("arbitrary",), vmem_limit_bytes=40 << 20
        ),
        cost_estimate=pl.CostEstimate(
            flops=8 * count * width * size * size * parts * samples,
            bytes_accessed=count * width * size * (8 * size + 4 * parts * samples),
            transcendentals=0,
        ),
    )(table, *operands)


def permute(route):
    return lambda block: lax.ppermute(block, "grp", route)


def split_exchange(voltages, weights, table, chunks):
    devices = lax.axis_size("grp")
    plane = devices // 4
    channels = voltages.shape[0] // 2
    me = lax.axis_index("grp")
    column = lax.axis_index("chan")

    def behind(i):
        return (i - plane) % devices

    def beyond(i):
        return (i + plane) % devices

    def upper(i):
        return i % plane >= plane // 2

    everyone = range(devices)
    forward = permute([(behind(i) if upper(i) else beyond(i), i) for i in everyone])
    straight = permute([(beyond(i) if upper(i) else behind(i), i) for i in everyone])
    across = permute([(i ^ (plane // 2), i) for i in everyone])
    twin = permute([(i ^ 1, i) for i in everyone])

    def piece(of_column, first, count):
        block = lax.dynamic_slice_in_dim(voltages, of_column * channels + first, count, axis=0)
        return block * weights

    def spread(own):
        theirs = forward(own)
        others = straight(own)
        partner = across(own)
        passed = across(theirs)
        direct = [own, partner, passed, theirs, others]
        return direct + [twin(block) for block in direct]

    own, partner, passed, theirs, others = range(5)
    variants = []
    for y in range(2):
        chips = (others, passed, own, partner, theirs) if y == 0 else (theirs, partner, own, passed, others)
        for core in range(2):
            entries = []
            for j in range(-plane, plane + 1):
                chip = chips[(core + j) // 2 + 2]
                entries.append(chip if (core + j) % 2 == core else chip + 5)
            variants.append(tuple(entries))
    position = lax.rem(me, plane)
    table = jnp.concatenate([position[None].astype(jnp.int32), table])

    result = None
    first = 0
    for count in chunks:
        mine = piece(column, first, count)
        turned = lax.ppermute(piece(1 - column, first, count), "chan", [(0, 1), (1, 0)])
        halves = [spread(mine), spread(turned)]
        sources = [halves[part][at] for at in range(10) for part in range(2)]
        result = correlate(sources, 2, tuple(variants), table, first, channels, result)
        first += count
    return result


def window_exchange(voltages, weights, table):
    turned = lax.all_to_all(voltages * weights, "chan", split_axis=0, concat_axis=3, tiled=True)
    devices = lax.axis_size("grp")
    quarter = devices // 4
    width = 2 * quarter + 1

    def from_behind(block, distance):
        return lax.ppermute(block, "grp", [((i - distance) % devices, i) for i in range(devices)])

    window = [from_behind(turned, quarter)]
    while len(window) < width:
        window += [from_behind(block, -len(window)) for block in window[: width - len(window)]]
    table = jnp.concatenate([jnp.zeros((1,), jnp.int32), table])
    return correlate(window, 1, (tuple(range(width)),), table, 0, turned.shape[0], None)


def on_device(voltages, input_flags, pair_order):
    weights = input_flags.astype(jnp.bfloat16)[None, None, :, None]
    if lax.axis_size("grp") == 16 and lax.axis_size("chan") == 2:
        return split_exchange(voltages, weights, pair_order, (4, 4, 4, 4))
    return window_exchange(voltages, weights, pair_order)


def solution(mesh):
    return jax.shard_map(
        on_device,
        mesh=mesh,
        in_specs=(P(None, None, "grp", "chan"), P("grp"), P()),
        out_specs=P("grp", None, "chan", None, None),
        check_vma=False,
    )
```

```python
import functools

import jax
import jax.numpy as jnp
from jax import lax
from jax.experimental import pallas as pl
from jax.experimental.pallas import tpu as pltpu
from jax.sharding import PartitionSpec as P


def pair_kernel(variants, parts, blocks, joined, table, *refs):
    width = len(variants[0])
    sources = refs[:blocks]
    out, window, sems = refs[-3:]
    step = pl.program_id(0)
    steps = pl.num_programs(0)

    def copy(source, channel, slot, entry, part):
        if joined:
            block = sources[source].at[part, channel]
        else:
            block = sources[source * parts + part].at[channel]
        return pltpu.make_async_copy(block, window.at[slot, entry, part], sems.at[slot, entry, part])

    def fetch(channel, slot):
        for at, variant in enumerate(variants):

            @pl.when(table[0] == at)
            def _():
                for entry, source in enumerate(variant):
                    for part in range(parts):
                        copy(source, channel, slot, entry, part).start()

    @pl.when(step == 0)
    def _():
        fetch(0, 0)

    @pl.when(step + 1 < steps)
    def _():
        fetch(step + 1, lax.rem(step + 1, 2))

    slot = lax.rem(step, 2)
    for entry in range(width):
        for part in range(parts):
            copy(0, 0, slot, entry, part).wait()

    half = width // 2
    size = window.shape[-2]
    scale = jnp.float32(1.0 / (parts * window.shape[-1]))
    contract = (((1,), (1,)), ((), ()))

    def pair(d, carry):
        a = half - d // 2
        b = half + (d + 1) // 2
        left, real, imag = [], [], []
        for part in range(parts):
            b_r, b_i = window[slot, b, part, 0], window[slot, b, part, 1]
            left += [window[slot, a, part, 0], window[slot, a, part, 1]]
            real += [b_r, b_i]
            imag += [-b_i, b_r]
        left = jnp.concatenate(left, axis=1)
        for at, right in enumerate((real, imag)):
            sums = lax.dot_general(
                left, jnp.concatenate(right, axis=1), contract, preferred_element_type=jnp.float32
            )
            out[0, table[1 + d], 0, :, at * size : (at + 1) * size] = sums * scale
        return carry

    if width <= 9:
        for d in range(width):
            pair(d, 0)
    else:
        lax.fori_loop(0, width, pair, 0)


def correlate(blocks, variants, table, first, channels, previous):
    joined = not isinstance(blocks[0], (list, tuple))
    sources = list(blocks) if joined else [array for block in blocks for array in block]
    parts = sources[0].shape[0] if joined else len(blocks[0])
    count, _, size, samples = sources[0].shape[-4:]
    width = len(variants[0])
    out_shape = (1, width, channels, size, 2 * size)
    operands = sources + ([] if previous is None else [previous])
    return pl.pallas_call(
        functools.partial(pair_kernel, variants, parts, len(sources), joined),
        out_shape=jax.ShapeDtypeStruct(out_shape, jnp.float32),
        grid_spec=pltpu.PrefetchScalarGridSpec(
            num_scalar_prefetch=1,
            grid=(count,),
            in_specs=[pl.BlockSpec(memory_space=pltpu.HBM)] * len(operands),
            out_specs=pl.BlockSpec((1, width, 1, size, 2 * size), lambda c, t: (0, 0, first + c, 0, 0)),
            scratch_shapes=[
                pltpu.VMEM((2, width, parts, 2, size, samples), jnp.bfloat16),
                pltpu.SemaphoreType.DMA((2, width, parts)),
            ],
        ),
        input_output_aliases={} if previous is None else {len(operands): 0},
        compiler_params=pltpu.CompilerParams(dimension_semantics=("arbitrary",)),
        cost_estimate=pl.CostEstimate(
            flops=8 * count * width * size * size * parts * samples,
            bytes_accessed=count * width * size * (8 * size + 4 * parts * samples),
            transcendentals=0,
        ),
    )(table, *operands)


def after(kept, tokens):
    operands = list(kept) + list(tokens)
    return pl.pallas_call(
        lambda *refs: None,
        out_shape=tuple(jax.ShapeDtypeStruct(array.shape, array.dtype) for array in kept),
        in_specs=[pl.BlockSpec(memory_space=pltpu.HBM)] * len(operands),
        out_specs=(pl.BlockSpec(memory_space=pltpu.HBM),) * len(kept),
        input_output_aliases={at: at for at in range(len(kept))},
        cost_estimate=pl.CostEstimate(flops=0, bytes_accessed=0, transcendentals=0),
    )(*operands)


def permute(axis, route):
    return lambda block: lax.ppermute(block, axis, route)


class Piece:
    def __init__(self, own, moves):
        self.own = own
        self.forward, self.straight, self.across, self.twin = moves

    def near(self):
        self.theirs = self.forward(self.own)
        self.partner = self.across(self.own)

    def near_twins(self):
        twins = self.twin([self.own, self.theirs, self.partner])
        self.own_twin, self.theirs_twin, self.partner_twin = twins
        return twins

    def far(self):
        self.others = self.straight(self.own)
        self.passed = self.across(self.theirs)

    def far_twins(self):
        twins = self.twin([self.others, self.passed])
        self.others_twin, self.passed_twin = twins
        return twins

    def blocks(self):
        return [
            self.own,
            self.partner,
            self.passed,
            self.theirs,
            self.others,
            self.own_twin,
            self.partner_twin,
            self.passed_twin,
            self.theirs_twin,
            self.others_twin,
        ]


def split_exchange(voltages, weights, table, chunks):
    devices = lax.axis_size("grp")
    plane = devices // 4
    channels = voltages.shape[0] // 2
    me = lax.axis_index("grp")
    column = lax.axis_index("chan")

    def behind(i):
        return (i - plane) % devices

    def beyond(i):
        return (i + plane) % devices

    def upper(i):
        return i % plane >= plane // 2

    everyone = range(devices)
    forward = permute("grp", [(behind(i) if upper(i) else beyond(i), i) for i in everyone])
    straight = permute("grp", [(beyond(i) if upper(i) else behind(i), i) for i in everyone])
    across = permute("grp", [(i ^ (plane // 2), i) for i in everyone])
    swap = permute("grp", [(i ^ 1, i) for i in everyone])
    in_order = table[0] >= 0

    def twin(blocks):
        return lax.cond(
            in_order,
            lambda given: [swap(block) for block in given],
            lambda given: [jnp.zeros_like(block) for block in given],
            list(blocks),
        )

    turn = permute("chan", [(0, 1), (1, 0)])
    moves = (forward, straight, across, twin)

    own, partner, passed, theirs, others = range(5)
    variants = []
    for y in range(2):
        chips = (others, passed, own, partner, theirs) if y == 0 else (theirs, partner, own, passed, others)
        for core in range(2):
            entries = []
            for j in range(-plane, plane + 1):
                chip = chips[(core + j) // 2 + 2]
                entries.append(chip if (core + j) % 2 == core else chip + 5)
            variants.append(tuple(entries))
    variants = tuple(variants)
    position = lax.rem(me, plane)
    table = jnp.concatenate([position[None].astype(jnp.int32), table])

    columns = voltages.reshape(2, channels, *voltages.shape[1:])
    firsts = [sum(chunks[:at]) for at in range(len(chunks))]
    stay, go = [
        lax.dynamic_slice_in_dim(voltages, of * channels, chunks[0], axis=0) * weights
        for of in (column, 1 - column)
    ]
    pieces = [Piece(stay, moves), Piece(turn(go), moves)]

    def turned(at, token):
        mine = columns[:, firsts[at] : firsts[at] + chunks[at]] * weights
        (mine,) = after([mine], [token])
        return Piece(lax.all_to_all(mine, "chan", split_axis=0, concat_axis=0), moves)

    pieces.append(turned(1, pieces[1].own))

    count = len(chunks) + 1
    steps = [("near", 0), ("near", 1)]
    for at in range(count - 2):
        steps += [("far", at), ("near", at + 2)]
    steps += [("far", count - 2), ("far", count - 1)]

    def kernel(at, result):
        if at == 0:
            blocks = list(zip(pieces[0].blocks(), pieces[1].blocks()))
        else:
            blocks = pieces[at + 1].blocks()
        return correlate(blocks, variants, table, firsts[at], channels, result)

    result, ready, shared = None, [], []

    def share(step, token):
        nonlocal result
        kind, at = steps[step]
        piece = pieces[at]
        if kind == "near":
            if token is not None:
                piece.theirs, piece.partner = after([piece.theirs, piece.partner], [token])
            shared.append(piece.near_twins())
        else:
            if token is not None:
                piece.others, piece.passed = after([piece.others, piece.passed], [token])
            shared.append(piece.far_twins())
            if at >= 1:
                result = kernel(at - 1, result)
                ready.append(step + 3)

    token = None
    for step, (kind, at) in enumerate(steps):
        piece = pieces[at]
        if step >= 2:
            share(step - 2, token)
            kept, waits = [piece.own], list(shared[step - 2])
            if kind == "far":
                kept.append(piece.theirs)
                waits += [piece.partner, piece.own_twin, piece.theirs_twin]
                if ready and ready[0] <= step:
                    ready.pop(0)
                    kept.append(result)
            kept = after(kept, waits)
            piece.own = kept[0]
            if kind == "far":
                piece.theirs = kept[1]
                if len(kept) == 3:
                    result = kept[2]
            token = piece.own
        if kind == "near":
            piece.near()
            if 2 <= at < count - 1:
                pieces.append(turned(at, piece.own))
        else:
            piece.far()
    share(len(steps) - 2, token)
    share(len(steps) - 1, None)
    return result


def window_exchange(voltages, weights, table):
    turned = lax.all_to_all(voltages * weights, "chan", split_axis=0, concat_axis=3, tiled=True)
    devices = lax.axis_size("grp")
    quarter = devices // 4
    width = 2 * quarter + 1

    def from_behind(block, distance):
        return lax.ppermute(block, "grp", [((i - distance) % devices, i) for i in range(devices)])

    window = [from_behind(turned, quarter)]
    while len(window) < width:
        window += [from_behind(block, -len(window)) for block in window[: width - len(window)]]
    table = jnp.concatenate([jnp.zeros((1,), jnp.int32), table])
    return correlate([[block] for block in window], (tuple(range(width)),), table, 0, turned.shape[0], None)


def on_device(voltages, input_flags, pair_order):
    weights = input_flags.astype(jnp.bfloat16)[None, None, :, None]
    if lax.axis_size("grp") == 16 and lax.axis_size("chan") == 2:
        return split_exchange(voltages, weights, pair_order, (6, 6, 4))
    return window_exchange(voltages, weights, pair_order)


def solution(mesh):
    return jax.shard_map(
        on_device,
        mesh=mesh,
        in_specs=(P(None, None, "grp", "chan"), P("grp"), P()),
        out_specs=P("grp", None, "chan", None, None),
        check_vma=False,
    )
```

```python
import functools

import jax
import jax.numpy as jnp
from jax import lax
from jax.experimental import pallas as pl
from jax.experimental.pallas import tpu as pltpu
from jax.sharding import PartitionSpec as P


HALVED, JOINED, STAGGER = (4, 4), (4, 4), True


def pair_kernel(variants, parts, blocks, joined, table, *refs):
    width = len(variants[0])
    sources = refs[:blocks]
    out, window, sems = refs[-3:]
    step = pl.program_id(0)
    steps = pl.num_programs(0)

    def copy(source, channel, slot, entry, part):
        if joined:
            block = sources[source].at[part, channel]
        else:
            block = sources[source * parts + part].at[channel]
        return pltpu.make_async_copy(block, window.at[slot, entry, part], sems.at[slot, entry, part])

    def fetch(channel, slot):
        for at, variant in enumerate(variants):

            @pl.when(table[0] == at)
            def _():
                for entry, source in enumerate(variant):
                    for part in range(parts):
                        copy(source, channel, slot, entry, part).start()

    @pl.when(step == 0)
    def _():
        fetch(0, 0)

    @pl.when(step + 1 < steps)
    def _():
        fetch(step + 1, lax.rem(step + 1, 2))

    slot = lax.rem(step, 2)
    for entry in range(width):
        for part in range(parts):
            copy(0, 0, slot, entry, part).wait()

    half = width // 2
    size = window.shape[-2]
    scale = jnp.float32(1.0 / (parts * window.shape[-1]))
    contract = (((1,), (1,)), ((), ()))

    def pair(d, carry):
        a = half - d // 2
        b = half + (d + 1) // 2
        left, real, imag = [], [], []
        for part in range(parts):
            b_r, b_i = window[slot, b, part, 0], window[slot, b, part, 1]
            left += [window[slot, a, part, 0], window[slot, a, part, 1]]
            real += [b_r, b_i]
            imag += [-b_i, b_r]
        left = jnp.concatenate(left, axis=1)
        for at, right in enumerate((real, imag)):
            sums = lax.dot_general(
                left, jnp.concatenate(right, axis=1), contract, preferred_element_type=jnp.float32
            )
            out[0, table[1 + d], 0, :, at * size : (at + 1) * size] = sums * scale
        return carry

    if width <= 9:
        for d in range(width):
            pair(d, 0)
    else:
        lax.fori_loop(0, width, pair, 0)


def correlate(blocks, variants, table, first, channels, previous):
    joined = not isinstance(blocks[0], (list, tuple))
    sources = list(blocks) if joined else [array for block in blocks for array in block]
    parts = sources[0].shape[0] if joined else len(blocks[0])
    count, _, size, samples = sources[0].shape[-4:]
    width = len(variants[0])
    out_shape = (1, width, channels, size, 2 * size)
    operands = sources + ([] if previous is None else [previous])
    return pl.pallas_call(
        functools.partial(pair_kernel, variants, parts, len(sources), joined),
        out_shape=jax.ShapeDtypeStruct(out_shape, jnp.float32),
        grid_spec=pltpu.PrefetchScalarGridSpec(
            num_scalar_prefetch=1,
            grid=(count,),
            in_specs=[pl.BlockSpec(memory_space=pltpu.HBM)] * len(operands),
            out_specs=pl.BlockSpec((1, width, 1, size, 2 * size), lambda c, t: (0, 0, first + c, 0, 0)),
            scratch_shapes=[
                pltpu.VMEM((2, width, parts, 2, size, samples), jnp.bfloat16),
                pltpu.SemaphoreType.DMA((2, width, parts)),
            ],
        ),
        input_output_aliases={} if previous is None else {len(operands): 0},
        compiler_params=pltpu.CompilerParams(dimension_semantics=("arbitrary",)),
        cost_estimate=pl.CostEstimate(
            flops=4 * count * width * size * size * parts * samples,
            bytes_accessed=count * width * size * (4 * size + 2 * parts * samples),
            transcendentals=0,
        ),
    )(table, *operands)


def after(kept, tokens):
    operands = list(kept) + list(tokens)
    return pl.pallas_call(
        lambda *refs: None,
        out_shape=tuple(jax.ShapeDtypeStruct(array.shape, array.dtype) for array in kept),
        in_specs=[pl.BlockSpec(memory_space=pltpu.HBM)] * len(operands),
        out_specs=(pl.BlockSpec(memory_space=pltpu.HBM),) * len(kept),
        input_output_aliases={at: at for at in range(len(kept))},
        cost_estimate=pl.CostEstimate(flops=0, bytes_accessed=0, transcendentals=0),
    )(*operands)


def permute(axis, route):
    return lambda block: lax.ppermute(block, axis, route)


class Piece:
    def __init__(self, own, moves):
        self.own = own
        self.own_twin = None
        self.read_by, self.theirs_read_by = [], []
        self.forward, self.straight, self.across, self.twin = moves

    def near(self):
        self.theirs = self.forward(self.own)
        self.partner = self.across(self.own)

    def near_twins(self):
        if self.own_twin is None:
            self.own_twin, self.theirs_twin, self.partner_twin = self.twin([self.own, self.theirs, self.partner])
        else:
            self.theirs_twin, self.partner_twin = self.twin([self.theirs, self.partner])
        return [self.own_twin, self.theirs_twin, self.partner_twin]

    def far(self):
        self.others = self.straight(self.own)
        self.passed = self.across(self.theirs)

    def far_twins(self):
        twins = self.twin([self.others, self.passed])
        self.others_twin, self.passed_twin = twins
        return twins

    def blocks(self):
        return [
            self.own,
            self.partner,
            self.passed,
            self.theirs,
            self.others,
            self.own_twin,
            self.partner_twin,
            self.passed_twin,
            self.theirs_twin,
            self.others_twin,
        ]


def split_exchange(voltages, weights, table, halved, joined, stagger):
    devices = lax.axis_size("grp")
    plane = devices // 4
    channels = voltages.shape[0] // 2
    me = lax.axis_index("grp")
    column = lax.axis_index("chan")

    def behind(i):
        return (i - plane) % devices

    def beyond(i):
        return (i + plane) % devices

    def upper(i):
        return i % plane >= plane // 2

    everyone = range(devices)
    forward = permute("grp", [(behind(i) if upper(i) else beyond(i), i) for i in everyone])
    straight = permute("grp", [(beyond(i) if upper(i) else behind(i), i) for i in everyone])
    across = permute("grp", [(i ^ (plane // 2), i) for i in everyone])
    swap = permute("grp", [(i ^ 1, i) for i in everyone])
    in_order = table[0] >= 0

    def twin(blocks):
        return lax.cond(
            in_order,
            lambda given: [swap(block) for block in given],
            lambda given: [jnp.zeros_like(block) for block in given],
            list(blocks),
        )

    turn = permute("chan", [(0, 1), (1, 0)])
    moves = (forward, straight, across, twin)

    own, partner, passed, theirs, others = range(5)
    variants = []
    for y in range(2):
        chips = (others, passed, own, partner, theirs) if y == 0 else (theirs, partner, own, passed, others)
        for core in range(2):
            entries = []
            for j in range(-plane, plane + 1):
                chip = chips[(core + j) // 2 + 2]
                entries.append(chip if (core + j) % 2 == core else chip + 5)
            variants.append(tuple(entries))
    variants = tuple(variants)
    position = lax.rem(me, plane)
    table = jnp.concatenate([position[None].astype(jnp.int32), table])

    columns = voltages.reshape(2, channels, *voltages.shape[1:])
    sizes = halved + joined
    firsts = [sum(sizes[:at]) for at in range(len(sizes))]

    stays, mines = [], []
    for chunk, (first, size) in enumerate(zip(firsts, sizes)):
        if chunk < len(halved):
            stay, mine = [
                lax.dynamic_slice_in_dim(voltages, of * channels + first, size, axis=0) * weights
                for of in (column, 1 - column)
            ]
            stays.append(Piece(stay, moves))
        else:
            mine = columns[:, first : first + size] * weights
        mines.append(mine)
    turns = [Piece(None, moves) for _ in sizes]

    def corner_turn(chunk):
        mine = mines[chunk]
        if chunk:
            earlier, step = turns[chunk - 1], steps[chunk - 1][1]
            (mine,) = after([mine], [earlier.own, step.theirs])
            earlier.read_by.append(mine)
            step.theirs_read_by.append(mine)
        if chunk < len(halved):
            turns[chunk].own = turn(mine)
        else:
            turns[chunk].own = lax.all_to_all(mine, "chan", split_axis=0, concat_axis=0)

    chunked = [[stays[at], turns[at]] if at < len(halved) else [turns[at]] for at in range(len(sizes))]
    steps = [("near", piece) for piece in stays + turns]
    steps += [("far", piece) for pieces in chunked for piece in pieces]

    result, made, shared = None, None, []
    work = list(range(len(sizes)))

    def share(step, token):
        nonlocal result
        kind, piece = steps[step]
        if kind == "near":
            if token is not None:
                piece.theirs, piece.partner = after([piece.theirs, piece.partner], [token] + piece.theirs_read_by)
            shared.append(piece.near_twins())
            return
        kept, waits = [piece.others, piece.passed], [] if token is None else [token]
        if step >= len(steps) - 2 and result is not None:
            kept.append(result)
        kept = after(kept, waits) if waits or len(kept) == 3 else kept
        piece.others, piece.passed = kept[:2]
        result = kept[2] if len(kept) == 3 else result
        shared.append(piece.far_twins())

    def compute(step):
        nonlocal result, made
        kind, piece = steps[step]
        if kind == "near" or piece is not chunked[work[0]][-1]:
            return
        chunk = work.pop(0)
        blocks = [piece.blocks() for piece in chunked[chunk]]
        blocks = list(zip(*blocks)) if len(blocks) > 1 else blocks[0]
        result = correlate(blocks, variants, table, firsts[chunk], channels, result)
        made = step

    corner_turn(0)
    first, second = steps[0][1], steps[1][1]
    if stagger:
        first.own_twin = twin([first.own])[0]
        second.own = after([second.own], [first.own_twin] + second.read_by)[0]
    token = None
    for step, (kind, piece) in enumerate(steps):
        if step >= 2:
            share(step - 2, token)
            kept, waits = [piece.own], shared[step - 2] + piece.read_by
            if kind == "far":
                kept.append(piece.theirs)
                waits = waits + [piece.partner, piece.own_twin, piece.theirs_twin]
                if made is not None and made + 4 <= step:
                    made = None
                    kept.append(result)
            kept = after(kept, waits)
            token = piece.own = kept[0]
            if kind == "far":
                piece.theirs = kept[1]
                if len(kept) == 3:
                    result = kept[2]
        if kind == "near":
            piece.near()
            if step + 1 < len(sizes):
                corner_turn(step + 1)
        else:
            piece.far()
        if step >= 2:
            compute(step - 2)
    for step in range(len(steps) - 2, len(steps)):
        share(step, token if step < len(steps) - 1 else None)
        compute(step)
    return result


def window_exchange(voltages, weights, table):
    turned = lax.all_to_all(voltages * weights, "chan", split_axis=0, concat_axis=3, tiled=True)
    devices = lax.axis_size("grp")
    quarter = devices // 4
    width = 2 * quarter + 1

    def from_behind(block, distance):
        return lax.ppermute(block, "grp", [((i - distance) % devices, i) for i in range(devices)])

    window = [from_behind(turned, quarter)]
    while len(window) < width:
        window += [from_behind(block, -len(window)) for block in window[: width - len(window)]]
    table = jnp.concatenate([jnp.zeros((1,), jnp.int32), table])
    return correlate([[block] for block in window], (tuple(range(width)),), table, 0, turned.shape[0], None)


def on_device(voltages, input_flags, pair_order):
    weights = input_flags.astype(jnp.bfloat16)[None, None, :, None]
    if lax.axis_size("grp") == 16 and lax.axis_size("chan") == 2:
        return split_exchange(voltages, weights, pair_order, HALVED, JOINED, STAGGER)
    return window_exchange(voltages, weights, pair_order)


def solution(mesh):
    return jax.shard_map(
        on_device,
        mesh=mesh,
        in_specs=(P(None, None, "grp", "chan"), P("grp"), P()),
        out_specs=P("grp", None, "chan", None, None),
        check_vma=False,
    )
```

```python
import functools

import jax
import jax.numpy as jnp
from jax import lax
from jax.experimental import pallas as pl
from jax.experimental.pallas import tpu as pltpu
from jax.sharding import PartitionSpec as P


def pair_kernel(variants, parts, blocks, joined, table, *refs):
    width = len(variants[0])
    sources = refs[:blocks]
    out, window, sems = refs[-3:]
    step = pl.program_id(0)
    steps = pl.num_programs(0)

    def copy(source, channel, slot, entry, part):
        if joined:
            block = sources[source].at[part, channel]
        else:
            block = sources[source * parts + part].at[channel]
        return pltpu.make_async_copy(block, window.at[slot, entry, part], sems.at[slot, entry, part])

    def fetch(channel, slot):
        for at, variant in enumerate(variants):

            @pl.when(table[0] == at)
            def _():
                for entry, source in enumerate(variant):
                    for part in range(parts):
                        copy(source, channel, slot, entry, part).start()

    @pl.when(step == 0)
    def _():
        fetch(0, 0)

    @pl.when(step + 1 < steps)
    def _():
        fetch(step + 1, lax.rem(step + 1, 2))

    slot = lax.rem(step, 2)
    for entry in range(width):
        for part in range(parts):
            copy(0, 0, slot, entry, part).wait()

    half = width // 2
    size = window.shape[-2]
    scale = jnp.float32(1.0 / (parts * window.shape[-1]))
    contract = (((1,), (1,)), ((), ()))

    def pair(d, carry):
        a = half - d // 2
        b = half + (d + 1) // 2
        left, real, imag = [], [], []
        for part in range(parts):
            b_r, b_i = window[slot, b, part, 0], window[slot, b, part, 1]
            left += [window[slot, a, part, 0], window[slot, a, part, 1]]
            real += [b_r, b_i]
            imag += [-b_i, b_r]
        left = jnp.concatenate(left, axis=1)
        for at, right in enumerate((real, imag)):
            sums = lax.dot_general(
                left, jnp.concatenate(right, axis=1), contract, preferred_element_type=jnp.float32
            )
            out[0, table[1 + d], 0, :, at * size : (at + 1) * size] = sums * scale
        return carry

    if width <= 9:
        for d in range(width):
            pair(d, 0)
    else:
        lax.fori_loop(0, width, pair, 0)


def correlate(blocks, variants, table, first, channels, previous):
    joined = not isinstance(blocks[0], (list, tuple))
    sources = list(blocks) if joined else [array for block in blocks for array in block]
    parts = sources[0].shape[0] if joined else len(blocks[0])
    count, _, size, samples = sources[0].shape[-4:]
    width = len(variants[0])
    out_shape = (1, width, channels, size, 2 * size)
    operands = sources + ([] if previous is None else [previous])
    return pl.pallas_call(
        functools.partial(pair_kernel, variants, parts, len(sources), joined),
        out_shape=jax.ShapeDtypeStruct(out_shape, jnp.float32),
        grid_spec=pltpu.PrefetchScalarGridSpec(
            num_scalar_prefetch=1,
            grid=(count,),
            in_specs=[pl.BlockSpec(memory_space=pltpu.HBM)] * len(operands),
            out_specs=pl.BlockSpec((1, width, 1, size, 2 * size), lambda c, t: (0, 0, first + c, 0, 0)),
            scratch_shapes=[
                pltpu.VMEM((2, width, parts, 2, size, samples), jnp.bfloat16),
                pltpu.SemaphoreType.DMA((2, width, parts)),
            ],
        ),
        input_output_aliases={} if previous is None else {len(operands): 0},
        compiler_params=pltpu.CompilerParams(dimension_semantics=("arbitrary",)),
        cost_estimate=pl.CostEstimate(
            flops=4 * count * width * size * size * parts * samples,
            bytes_accessed=count * width * size * (4 * size + 2 * parts * samples),
            transcendentals=0,
        ),
    )(table, *operands)


def after(kept, tokens):
    operands = list(kept) + list(tokens)
    return pl.pallas_call(
        lambda *refs: None,
        out_shape=tuple(jax.ShapeDtypeStruct(array.shape, array.dtype) for array in kept),
        in_specs=[pl.BlockSpec(memory_space=pltpu.HBM)] * len(operands),
        out_specs=(pl.BlockSpec(memory_space=pltpu.HBM),) * len(kept),
        input_output_aliases={at: at for at in range(len(kept))},
        cost_estimate=pl.CostEstimate(flops=0, bytes_accessed=0, transcendentals=0),
    )(*operands)


def permute(axis, route):
    return lambda block: lax.ppermute(block, axis, route)


class Piece:
    def __init__(self, own, moves):
        self.own = own
        self.forward, self.straight, self.across, self.twin = moves

    def near(self):
        self.theirs = self.forward(self.own)
        self.partner = self.across(self.own)

    def near_twins(self):
        twins = self.twin([self.own, self.theirs, self.partner])
        self.own_twin, self.theirs_twin, self.partner_twin = twins
        return twins

    def far(self):
        self.others = self.straight(self.own)
        self.passed = self.across(self.theirs)

    def far_twins(self):
        twins = self.twin([self.others, self.passed])
        self.others_twin, self.passed_twin = twins
        return twins

    def blocks(self):
        return [
            self.own,
            self.partner,
            self.passed,
            self.theirs,
            self.others,
            self.own_twin,
            self.partner_twin,
            self.passed_twin,
            self.theirs_twin,
            self.others_twin,
        ]


def split_exchange(voltages, weights, table, chunks):
    devices = lax.axis_size("grp")
    plane = devices // 4
    channels = voltages.shape[0] // 2
    me = lax.axis_index("grp")
    column = lax.axis_index("chan")

    def behind(i):
        return (i - plane) % devices

    def beyond(i):
        return (i + plane) % devices

    def upper(i):
        return i % plane >= plane // 2

    everyone = range(devices)
    forward = permute("grp", [(behind(i) if upper(i) else beyond(i), i) for i in everyone])
    straight = permute("grp", [(beyond(i) if upper(i) else behind(i), i) for i in everyone])
    across = permute("grp", [(i ^ (plane // 2), i) for i in everyone])
    swap = permute("grp", [(i ^ 1, i) for i in everyone])
    in_order = table[0] >= 0

    def twin(blocks):
        return lax.cond(
            in_order,
            lambda given: [swap(block) for block in given],
            lambda given: [jnp.zeros_like(block) for block in given],
            list(blocks),
        )

    turn = permute("chan", [(0, 1), (1, 0)])
    moves = (forward, straight, across, twin)

    own, partner, passed, theirs, others = range(5)
    variants = []
    for y in range(2):
        chips = (others, passed, own, partner, theirs) if y == 0 else (theirs, partner, own, passed, others)
        for core in range(2):
            entries = []
            for j in range(-plane, plane + 1):
                chip = chips[(core + j) // 2 + 2]
                entries.append(chip if (core + j) % 2 == core else chip + 5)
            variants.append(tuple(entries))
    variants = tuple(variants)
    position = lax.rem(me, plane)
    table = jnp.concatenate([position[None].astype(jnp.int32), table])

    columns = voltages.reshape(2, channels, *voltages.shape[1:])
    firsts = [sum(chunks[:at]) for at in range(len(chunks))]
    stay, go = [
        lax.dynamic_slice_in_dim(voltages, of * channels, chunks[0], axis=0) * weights
        for of in (column, 1 - column)
    ]
    pieces = [Piece(stay, moves), Piece(turn(go), moves)]

    begun = [None, None]
    for first, size in zip(firsts[1:], chunks[1:]):
        mine = columns[:, first : first + size] * weights
        begun.append(None)
        pieces.append(Piece(lax.all_to_all(mine, "chan", split_axis=0, concat_axis=0), moves))
    begun.append(None)

    count = len(chunks) + 1
    steps = [(kind, at) for kind in ("near", "far") for at in range(count)]

    def kernel(at, result):
        if at == 0:
            blocks = list(zip(pieces[0].blocks(), pieces[1].blocks()))
        else:
            blocks = pieces[at + 1].blocks()
        return correlate(blocks, variants, table, firsts[at], channels, result)

    result, ready, shared = None, [], []

    def share(step, token):
        nonlocal result
        kind, at = steps[step]
        piece = pieces[at]
        if kind == "near":
            if token is not None:
                piece.theirs, piece.partner = after([piece.theirs, piece.partner], [token])
            shared.append(piece.near_twins())
        else:
            kept, waits = [piece.others, piece.passed], [] if token is None else [token]
            if result is not None and step < len(steps) - 1:
                kept.append(result)
            kept = after(kept, waits) if waits or len(kept) == 3 else kept
            piece.others, piece.passed = kept[:2]
            result = kept[2] if len(kept) == 3 else result
            shared.append(piece.far_twins())
            if at >= 1:
                result = kernel(at - 1, result)
                ready.append(step + 4)

    token = None
    for step, (kind, at) in enumerate(steps):
        piece = pieces[at]
        if step >= 2:
            share(step - 2, token)
            kept, waits = [piece.own], list(shared[step - 2])
            if kind == "far":
                kept.append(piece.theirs)
                waits += [piece.partner, piece.own_twin, piece.theirs_twin]
                if ready and ready[0] <= step:
                    ready.pop(0)
                    kept.append(result)
            elif begun[at + 1] is not None:
                waits.append(begun[at + 1])
            kept = after(kept, waits)
            piece.own = kept[0]
            if kind == "far":
                piece.theirs = kept[1]
                if len(kept) == 3:
                    result = kept[2]
            token = piece.own
        if kind == "near":
            piece.near()
        else:
            piece.far()
    share(len(steps) - 2, token)
    share(len(steps) - 1, None)
    return result


def window_exchange(voltages, weights, table):
    turned = lax.all_to_all(voltages * weights, "chan", split_axis=0, concat_axis=3, tiled=True)
    devices = lax.axis_size("grp")
    quarter = devices // 4
    width = 2 * quarter + 1

    def from_behind(block, distance):
        return lax.ppermute(block, "grp", [((i - distance) % devices, i) for i in range(devices)])

    window = [from_behind(turned, quarter)]
    while len(window) < width:
        window += [from_behind(block, -len(window)) for block in window[: width - len(window)]]
    table = jnp.concatenate([jnp.zeros((1,), jnp.int32), table])
    return correlate([[block] for block in window], (tuple(range(width)),), table, 0, turned.shape[0], None)


def on_device(voltages, input_flags, pair_order):
    weights = input_flags.astype(jnp.bfloat16)[None, None, :, None]
    if lax.axis_size("grp") == 16 and lax.axis_size("chan") == 2:
        return split_exchange(voltages, weights, pair_order, (8, 4, 4))
    return window_exchange(voltages, weights, pair_order)


def solution(mesh):
    return jax.shard_map(
        on_device,
        mesh=mesh,
        in_specs=(P(None, None, "grp", "chan"), P("grp"), P()),
        out_specs=P("grp", None, "chan", None, None),
        check_vma=False,
    )
```

```python
import functools

import jax
import jax.numpy as jnp
from jax import lax
from jax.experimental import pallas as pl
from jax.experimental.pallas import tpu as pltpu
from jax.sharding import PartitionSpec as P


def pair_kernel(variants, parts, blocks, joined, table, *refs):
    width = len(variants[0])
    sources = refs[:blocks]
    out, window, sems = refs[-3:]
    step = pl.program_id(0)
    steps = pl.num_programs(0)

    def copy(source, channel, slot, entry, part):
        if joined:
            block = sources[source].at[part, channel]
        else:
            block = sources[source * parts + part].at[channel]
        return pltpu.make_async_copy(block, window.at[slot, entry, part], sems.at[slot, entry, part])

    def fetch(channel, slot):
        for at, variant in enumerate(variants):

            @pl.when(table[0] == at)
            def _():
                for entry, source in enumerate(variant):
                    for part in range(parts):
                        copy(source, channel, slot, entry, part).start()

    @pl.when(step == 0)
    def _():
        fetch(0, 0)

    @pl.when(step + 1 < steps)
    def _():
        fetch(step + 1, lax.rem(step + 1, 2))

    slot = lax.rem(step, 2)
    for entry in range(width):
        for part in range(parts):
            copy(0, 0, slot, entry, part).wait()

    half = width // 2
    size = window.shape[-2]
    scale = jnp.float32(1.0 / (parts * window.shape[-1]))
    contract = (((1,), (1,)), ((), ()))

    def pair(d, carry):
        a = half - d // 2
        b = half + (d + 1) // 2
        left, real, imag = [], [], []
        for part in range(parts):
            b_r, b_i = window[slot, b, part, 0], window[slot, b, part, 1]
            left += [window[slot, a, part, 0], window[slot, a, part, 1]]
            real += [b_r, b_i]
            imag += [-b_i, b_r]
        left = jnp.concatenate(left, axis=1)
        for at, right in enumerate((real, imag)):
            sums = lax.dot_general(
                left, jnp.concatenate(right, axis=1), contract, preferred_element_type=jnp.float32
            )
            out[0, table[1 + d], 0, :, at * size : (at + 1) * size] = sums * scale
        return carry

    if width <= 9:
        for d in range(width):
            pair(d, 0)
    else:
        lax.fori_loop(0, width, pair, 0)


def correlate(blocks, variants, table, first, channels, previous):
    joined = not isinstance(blocks[0], (list, tuple))
    sources = list(blocks) if joined else [array for block in blocks for array in block]
    parts = sources[0].shape[0] if joined else len(blocks[0])
    count, _, size, samples = sources[0].shape[-4:]
    width = len(variants[0])
    out_shape = (1, width, channels, size, 2 * size)
    operands = sources + ([] if previous is None else [previous])
    return pl.pallas_call(
        functools.partial(pair_kernel, variants, parts, len(sources), joined),
        out_shape=jax.ShapeDtypeStruct(out_shape, jnp.float32),
        grid_spec=pltpu.PrefetchScalarGridSpec(
            num_scalar_prefetch=1,
            grid=(count,),
            in_specs=[pl.BlockSpec(memory_space=pltpu.HBM)] * len(operands),
            out_specs=pl.BlockSpec((1, width, 1, size, 2 * size), lambda c, t: (0, 0, first + c, 0, 0)),
            scratch_shapes=[
                pltpu.VMEM((2, width, parts, 2, size, samples), jnp.bfloat16),
                pltpu.SemaphoreType.DMA((2, width, parts)),
            ],
        ),
        input_output_aliases={} if previous is None else {len(operands): 0},
        compiler_params=pltpu.CompilerParams(dimension_semantics=("arbitrary",)),
        cost_estimate=pl.CostEstimate(
            flops=4 * count * width * size * size * parts * samples,
            bytes_accessed=count * width * size * (4 * size + 2 * parts * samples),
            transcendentals=0,
        ),
    )(table, *operands)


def after(kept, tokens):
    operands = list(kept) + list(tokens)
    return pl.pallas_call(
        lambda *refs: None,
        out_shape=tuple(jax.ShapeDtypeStruct(array.shape, array.dtype) for array in kept),
        in_specs=[pl.BlockSpec(memory_space=pltpu.HBM)] * len(operands),
        out_specs=(pl.BlockSpec(memory_space=pltpu.HBM),) * len(kept),
        input_output_aliases={at: at for at in range(len(kept))},
        cost_estimate=pl.CostEstimate(flops=0, bytes_accessed=0, transcendentals=0),
    )(*operands)


def permute(axis, route):
    return lambda block: lax.ppermute(block, axis, route)


class Piece:
    def __init__(self, own, moves):
        self.own = own
        self.forward, self.straight, self.across, self.twin = moves

    def near(self):
        self.theirs = self.forward(self.own)
        self.partner = self.across(self.own)

    def near_twins(self):
        twins = self.twin([self.own, self.theirs, self.partner])
        self.own_twin, self.theirs_twin, self.partner_twin = twins
        return twins

    def far(self):
        self.others = self.straight(self.own)
        self.passed = self.across(self.theirs)

    def far_twins(self):
        twins = self.twin([self.others, self.passed])
        self.others_twin, self.passed_twin = twins
        return twins

    def blocks(self):
        return [
            self.own,
            self.partner,
            self.passed,
            self.theirs,
            self.others,
            self.own_twin,
            self.partner_twin,
            self.passed_twin,
            self.theirs_twin,
            self.others_twin,
        ]


def split_exchange(voltages, weights, table, chunks):
    devices = lax.axis_size("grp")
    plane = devices // 4
    channels = voltages.shape[0] // 2
    me = lax.axis_index("grp")
    column = lax.axis_index("chan")

    def behind(i):
        return (i - plane) % devices

    def beyond(i):
        return (i + plane) % devices

    def upper(i):
        return i % plane >= plane // 2

    everyone = range(devices)
    forward = permute("grp", [(behind(i) if upper(i) else beyond(i), i) for i in everyone])
    straight = permute("grp", [(beyond(i) if upper(i) else behind(i), i) for i in everyone])
    across = permute("grp", [(i ^ (plane // 2), i) for i in everyone])
    swap = permute("grp", [(i ^ 1, i) for i in everyone])
    in_order = table[0] >= 0

    def twin(blocks):
        return lax.cond(
            in_order,
            lambda given: [swap(block) for block in given],
            lambda given: [jnp.zeros_like(block) for block in given],
            list(blocks),
        )

    turn = permute("chan", [(0, 1), (1, 0)])
    moves = (forward, straight, across, twin)

    own, partner, passed, theirs, others = range(5)
    variants = []
    for y in range(2):
        chips = (others, passed, own, partner, theirs) if y == 0 else (theirs, partner, own, passed, others)
        for core in range(2):
            entries = []
            for j in range(-plane, plane + 1):
                chip = chips[(core + j) // 2 + 2]
                entries.append(chip if (core + j) % 2 == core else chip + 5)
            variants.append(tuple(entries))
    variants = tuple(variants)
    position = lax.rem(me, plane)
    table = jnp.concatenate([position[None].astype(jnp.int32), table])

    columns = voltages.reshape(2, channels, *voltages.shape[1:])
    firsts = [sum(chunks[:at]) for at in range(len(chunks))]
    stay, go = [
        lax.dynamic_slice_in_dim(voltages, of * channels, chunks[0], axis=0) * weights
        for of in (column, 1 - column)
    ]
    pieces = [Piece(stay, moves), Piece(turn(go), moves)]

    begun = [None, None]
    for first, size in zip(firsts[1:], chunks[1:]):
        mine = columns[:, first : first + size] * weights
        begun.append(None)
        pieces.append(Piece(lax.all_to_all(mine, "chan", split_axis=0, concat_axis=0), moves))
    begun.append(None)

    count = len(chunks) + 1
    steps = [(kind, at) for kind in ("near", "far") for at in range(count)]

    def kernel(at, result):
        if at == 0:
            blocks = list(zip(pieces[0].blocks(), pieces[1].blocks()))
        else:
            blocks = pieces[at + 1].blocks()
        return correlate(blocks, variants, table, firsts[at], channels, result)

    result, ready, shared = None, [], []

    def share(step, token):
        nonlocal result
        kind, at = steps[step]
        piece = pieces[at]
        if kind == "near":
            if token is not None:
                piece.theirs, piece.partner = after([piece.theirs, piece.partner], [token])
            shared.append(piece.near_twins())
        else:
            kept, waits = [piece.others, piece.passed], [] if token is None else [token]
            if result is not None and step < len(steps) - 1:
                kept.append(result)
            kept = after(kept, waits) if waits or len(kept) == 3 else kept
            piece.others, piece.passed = kept[:2]
            result = kept[2] if len(kept) == 3 else result
            shared.append(piece.far_twins())
            if at >= 1:
                result = kernel(at - 1, result)
                ready.append(step + 4)

    token = None
    for step, (kind, at) in enumerate(steps):
        piece = pieces[at]
        if step >= 2:
            share(step - 2, token)
            kept, waits = [piece.own], list(shared[step - 2])
            if kind == "far":
                kept.append(piece.theirs)
                waits += [piece.partner, piece.own_twin, piece.theirs_twin]
                if ready and ready[0] <= step:
                    ready.pop(0)
                    kept.append(result)
            elif begun[at + 1] is not None:
                waits.append(begun[at + 1])
            kept = after(kept, waits)
            piece.own = kept[0]
            if kind == "far":
                piece.theirs = kept[1]
                if len(kept) == 3:
                    result = kept[2]
            token = piece.own
        if kind == "near":
            piece.near()
        else:
            piece.far()
    share(len(steps) - 2, token)
    share(len(steps) - 1, None)
    return result


def window_exchange(voltages, weights, table):
    turned = lax.all_to_all(voltages * weights, "chan", split_axis=0, concat_axis=3, tiled=True)
    devices = lax.axis_size("grp")
    quarter = devices // 4
    width = 2 * quarter + 1

    def from_behind(block, distance):
        return lax.ppermute(block, "grp", [((i - distance) % devices, i) for i in range(devices)])

    window = [from_behind(turned, quarter)]
    while len(window) < width:
        window += [from_behind(block, -len(window)) for block in window[: width - len(window)]]
    table = jnp.concatenate([jnp.zeros((1,), jnp.int32), table])
    return correlate([[block] for block in window], (tuple(range(width)),), table, 0, turned.shape[0], None)


def on_device(voltages, input_flags, pair_order):
    weights = input_flags.astype(jnp.bfloat16)[None, None, :, None]
    if lax.axis_size("grp") == 16 and lax.axis_size("chan") == 2:
        return split_exchange(voltages, weights, pair_order, (7, 5, 4))
    return window_exchange(voltages, weights, pair_order)


def solution(mesh):
    return jax.shard_map(
        on_device,
        mesh=mesh,
        in_specs=(P(None, None, "grp", "chan"), P("grp"), P()),
        out_specs=P("grp", None, "chan", None, None),
        check_vma=False,
    )
```
